32 devices in a mesh: ctx: 8 (over z, y), kvh: 4 (over x, core).
Axes of the slice: x: 2, y: 2, z: 4, core: 2. Of those that a mesh axis runs over, the one named last changes fastest.
Arguments:
- queries: bfloat16 [4096, 3584], P('ctx', 'kvh'), may hold values from -384 to 384
- key_block: bfloat16 [4096, 512], P('ctx', 'kvh'), may hold values from -8 to 8
- value_block: bfloat16 [4096, 512], P('ctx', 'kvh'), may hold values from -6 to 6
- block_valid: int32 [8], replicated, may hold values from 2 to 512, as said below
- out_weight: bfloat16 [3584, 3584], P('kvh'), may hold values from -6 to 6
Outputs:
- projected: bfloat16 [4096, 3584], P(('ctx', 'kvh'))
The draws below stay inside these ranges and needn't reach their ends.
Inputs may be any that keep to these rules, and one draw needn't show every extreme that they name: `block_valid`: every entry but the last equals 512.
All inputs are finite; a program needn't handle non-finite values.
Results may differ from the reference program's by a relative error of at most 0.01.
Values may be sent and summed in bfloat16 or wider, within the bound.
No kernel may reach another device: no remote copies, remote signals or barrier semaphores. Data moves between devices by JAX's collectives and lax.ppermute only.
A program may use at most 128 MiB of HBM per device.

```python
import jax
import jax.numpy as jnp
from jax import lax

D = 3584
HD = 128
GROUP = 7
KV_HEADS = 4
BLK = 512
QDIM = 3584
TOKENS = 4096
N_CTX = 8


def joint_draw(key):
    block_count = N_CTX
    query_key, keys_key = jax.random.split(jax.random.fold_in(key, 7), 2)
    query_all = jax.random.truncated_normal(query_key, -4.0, 4.0, (block_count, BLK, KV_HEADS, GROUP, HD), jnp.float32)
    key_all = jax.random.truncated_normal(keys_key, -4.0, 4.0, (block_count, BLK, KV_HEADS, HD), jnp.float32)
    return (query_all, key_all)


def draw_queries(key, part):
    query_all, key_all = joint_draw(key)
    return query_all.reshape(N_CTX * BLK, KV_HEADS * GROUP * HD).astype(jnp.bfloat16)


def draw_key_block(key, part):
    query_all, key_all = joint_draw(key)
    return key_all.reshape(N_CTX * BLK, KV_HEADS * HD).astype(jnp.bfloat16)


def draw_block_valid(key, part):
    last_count = jax.random.randint(jax.random.fold_in(key, 11), (), 2, BLK + 1, jnp.int32)
    return jnp.full((N_CTX,), BLK, jnp.int32).at[N_CTX - 1].set(last_count)


def block_levels(rng, shape, cuts, low, top_value):
    loudness = 1.0
    for axis_at, shards_of in cuts:
        heights = jax.random.uniform(jax.random.fold_in(jax.random.fold_in(rng, 6), axis_at), (shards_of,), jnp.float32, low / len(cuts), top_value / len(cuts))
        loudness = loudness * jnp.repeat(jnp.exp(heights), shape[axis_at] // shards_of).reshape((-1,) + (1,) * (len(shape) - 1 - axis_at))
    return loudness


def bell_draw(own_key, dims, spread, bound, cuts=(), kind=jnp.bfloat16):
    gain = block_levels(own_key, dims, cuts, -0.22, 0.18) if cuts else 1.0
    array = jax.random.normal(own_key, dims, jnp.float32) * spread * gain
    return jnp.minimum(jnp.maximum(array, -bound), bound).astype(kind)


def setup_inputs(seed: int = 0) -> dict:
    streams_of = jax.random.split(jax.random.key(seed), 6)
    return {
        "queries": draw_queries(jax.random.fold_in(streams_of[5], 71), 0),
        "key_block": draw_key_block(jax.random.fold_in(streams_of[5], 71), 0),
        "value_block": bell_draw(streams_of[2], (TOKENS, KV_HEADS * HD), 1.0, 6.0, ((0, 8), (1, 4))),
        "block_valid": draw_block_valid(jax.random.fold_in(streams_of[5], 71), 0),
        "out_weight": bell_draw(streams_of[4], (QDIM, D), (max(1, QDIM // (7 * BLK))) ** -0.5, 6.0, ((0, 4),)),
    }


def reference(queries, key_block, value_block, block_valid, out_weight):
    block_count = N_CTX
    offsets = [1 << level_id for level_id in range((block_count - 1).bit_length())]
    query_all = queries.reshape(block_count, BLK, KV_HEADS, GROUP, HD)
    key_all = key_block.reshape(block_count, BLK, KV_HEADS, HD)
    value_all = value_block.reshape(block_count, BLK, KV_HEADS, HD)
    position = jnp.arange(BLK, dtype=jnp.int32)
    score_scale = HD ** -0.5

    def attend(block_id):
        key_list = [lax.dynamic_index_in_dim(key_all, block_id, 0, keepdims=False)]
        value_list = [lax.dynamic_index_in_dim(value_all, block_id, 0, keepdims=False)]
        mask_list = [(position[None, :] <= position[:, None]) & (position[None, :] < block_valid[block_id])]
        for offset in offsets:
            source = jnp.maximum(block_id - offset, 0).astype(jnp.int32)
            key_list.append(lax.dynamic_index_in_dim(key_all, source, 0, keepdims=False))
            value_list.append(lax.dynamic_index_in_dim(value_all, source, 0, keepdims=False))
            usable = (block_id - offset >= 0) & (position < block_valid[source])
            mask_list.append(jnp.broadcast_to(usable[None, :], (BLK, BLK)))
        keys_cat = jnp.concatenate(key_list, axis=0)
        values_cat = jnp.concatenate(value_list, axis=0)
        allowed = jnp.concatenate(mask_list, axis=1)
        query_now = lax.dynamic_index_in_dim(query_all, block_id, 0, keepdims=False)
        scores = jnp.einsum("qhgd,khd->hgqk", query_now.astype(jnp.float32), keys_cat.astype(jnp.float32)) * score_scale
        scores = jnp.where(allowed, scores, -1e30)
        row_max = jnp.max(scores, axis=-1, keepdims=True)
        numerators = jnp.where(allowed, jnp.exp(scores - row_max), 0.0)
        row_total = jnp.sum(numerators, axis=-1)
        weights = lax.optimization_barrier(numerators.astype(jnp.bfloat16))
        mixture = jnp.einsum("hgqk,khd->hgqd", weights.astype(jnp.float32), values_cat.astype(jnp.float32))
        mixture = mixture / row_total[..., None]
        return jnp.transpose(mixture, (2, 0, 1, 3)).reshape(BLK, KV_HEADS * GROUP * HD).astype(jnp.bfloat16)

    attended = lax.map(attend, jnp.arange(block_count, dtype=jnp.int32)).reshape(block_count * BLK, KV_HEADS * GROUP * HD)
    slab_width = GROUP * HD
    summed = jnp.zeros((attended.shape[0], out_weight.shape[1]), jnp.float32)
    for head_id in range(KV_HEADS):
        partial_value = jnp.dot(attended[:, head_id * slab_width:(head_id + 1) * slab_width],
                          out_weight[head_id * slab_width:(head_id + 1) * slab_width],
                          preferred_element_type=jnp.float32).astype(jnp.bfloat16)
        summed = summed + lax.optimization_barrier(partial_value).astype(jnp.float32)
    return summed.astype(jnp.bfloat16)
```

```python
import functools
import math

import jax
import jax.numpy as jnp
from jax import lax
from jax.experimental import pallas as pl
from jax.experimental.pallas import tpu as pltpu
from jax.sharding import PartitionSpec as P

F32 = jnp.float32
BF16 = jnp.bfloat16
LOW = -1e30
MIB = 1 << 20
CHUNKS = 2


def stack_heads(rows, head_size):
    heads = rows.shape[1] // head_size
    return jnp.concatenate(
        [rows[:, i * head_size : (i + 1) * head_size] for i in range(heads)], axis=0
    )


def unstack_heads(rows, heads):
    count = rows.shape[0] // heads
    return jnp.concatenate([rows[i * count : (i + 1) * count] for i in range(heads)], axis=1)


def block_step(q, keys, values, state, scale, limit=None, present=None):
    scores = lax.dot_general(q, keys, (((1,), (1,)), ((), ())), preferred_element_type=F32)
    if limit is not None:
        column = lax.broadcasted_iota(jnp.int32, scores.shape, 1)
        scores = jnp.where(column < limit, scores, LOW)
    block_max = jnp.max(scores, axis=1, keepdims=True)
    if present is not None:
        block_max = jnp.where(present, block_max, LOW)
    row_max = block_max if state is None else jnp.maximum(state[0], block_max)
    shift = row_max if present is None else jnp.where(present, row_max, -LOW)
    weights = jnp.exp2((scores - shift) * scale).astype(BF16)
    total = jnp.dot(weights, values, preferred_element_type=F32)
    if state is not None:
        total = total + state[1] * jnp.exp2((state[0] - row_max) * scale)
    return row_max, total


def gather_queries(q_ref, starts, count, head_size):
    return jnp.concatenate(
        [stack_heads(q_ref[pl.ds(start, count), :], head_size) for start in starts], axis=0
    )


def attend(q, state, k_refs, v_refs, wide, scale, limit, presents):
    block, head_size = k_refs[0].shape
    for i, v_ref in enumerate(v_refs):
        wide[i * block : (i + 1) * block, :head_size] = v_ref[...]
        wide[i * block : (i + 1) * block, head_size:] = jnp.ones((block, head_size), BF16)
    for i, k_ref in enumerate(k_refs):
        state = block_step(
            q,
            k_ref[...],
            wide[i * block : (i + 1) * block, :],
            state,
            scale,
            limit=limit if i == 0 else None,
            present=None if presents[i] is None else presents[i] > 0,
        )
    return state


def row_limits(starts, count, heads, valid):
    row = lax.broadcasted_iota(jnp.int32, (count, 1), 0)
    return jnp.concatenate(
        [jnp.minimum(row + (start + 1), valid) for start in starts for _ in range(heads)], axis=0
    )


def row_starts(turn, count, offset, piece):
    kvh_size = lax.axis_size("kvh")
    kvh_id = lax.axis_index("kvh")
    groups = kvh_size // 2
    lane = lax.rem(kvh_id, 2)
    target = lax.rem(lax.div(kvh_id, 2) + turn, groups)
    return [
        pl.multiple_of((target * 2 + part) * count + offset, piece) for part in (1 - lane, lane)
    ]


def stage_kernel(*refs):
    count = len(refs) // 2
    sems = refs[-1]
    copies = [
        pltpu.make_async_copy(refs[i], refs[count + i], sems.at[i]) for i in range(count)
    ]
    for copy in copies:
        copy.start()
    for copy in copies:
        copy.wait()


def stage(*arrays):
    return pl.pallas_call(
        stage_kernel,
        in_specs=[pl.BlockSpec(memory_space=pltpu.HBM)] * len(arrays),
        out_specs=[pl.BlockSpec(memory_space=pltpu.VMEM)] * len(arrays),
        out_shape=[jax.ShapeDtypeStruct(x.shape, x.dtype) for x in arrays],
        scratch_shapes=[pltpu.SemaphoreType.DMA((len(arrays),))],
        cost_estimate=pl.CostEstimate(
            flops=0, bytes_accessed=sum(2 * x.size for x in arrays), transcendentals=0
        ),
        compiler_params=pltpu.CompilerParams(vmem_limit_bytes=12 * MIB),
        name="stage",
    )(*arrays)


def kernel_body(mode, scale, levels, turn, offset, count, *refs):
    if mode != "late":
        block_valid, refs = refs[0], refs[1:]
    q_ref, refs = refs[0], refs[1:]
    if mode == "late":
        state_ref, refs = refs[0], refs[1:]
    if mode != "early":
        w_ref, refs = refs[0], refs[1:]
    blocks = len(levels)
    k_refs, refs = refs[:blocks], refs[blocks:]
    v_refs, refs = refs[:blocks], refs[blocks:]
    wide = refs[-1]
    head_size = k_refs[0].shape[1]
    heads = q_ref.shape[1] // head_size
    block_id = lax.axis_index("ctx")
    rows_of = q_ref.shape[0] // lax.axis_size("kvh")
    starts = row_starts(turn, rows_of, offset, count)
    q = gather_queries(q_ref, starts, count, head_size)
    presents = [None if level is None else block_id - (1 << level) + 1 for level in levels]
    limit, state = None, None
    if mode == "late":
        old = state_ref[:, :, offset : offset + count, :].reshape(2 * heads * count, -1)
        state = old[:, 3 * head_size // 2 :][:, :1], old
        state = (
            state[0],
            jnp.concatenate(
                [
                    old[:, :head_size],
                    jnp.broadcast_to(old[:, head_size:][:, :1], (old.shape[0], head_size)),
                ],
                axis=1,
            ),
        )
    else:
        limit = row_limits(starts, count, heads, block_valid[block_id])
    row_max, total = attend(q, state, k_refs, v_refs, wide, scale, limit, presents)
    if mode == "early":
        lane = lax.broadcasted_iota(jnp.int32, (1, 2 * head_size), 1)
        packed = jnp.where(lane < 3 * head_size // 2, total, row_max)
        refs[0][...] = packed.reshape(refs[0].shape)
        return
    mixed = (total[:, :head_size] / total[:, head_size:]).astype(BF16)
    half = heads * count
    mixed = jnp.concatenate([unstack_heads(mixed[i * half : (i + 1) * half], heads) for i in range(2)], axis=0)
    out = jnp.dot(mixed, w_ref[...], preferred_element_type=F32).astype(BF16)
    for part in range(2):
        refs[part][...] = out[part * count : (part + 1) * count]


def call(mode, scale, levels, turn, offset, count, block_valid, q, state, weight, keys, values):
    head_size = keys[0].shape[1]
    block = keys[0].shape[0]
    heads = q.shape[1] // head_size
    blocks = len(levels)
    operands = [q]
    if mode == "late":
        operands.append(state)
    if mode != "early":
        operands.append(weight)
    operands += list(keys) + list(values)
    if mode == "early":
        shapes = [jax.ShapeDtypeStruct((2, heads, count, 2 * head_size), F32)]
    else:
        shapes = [jax.ShapeDtypeStruct((count, weight.shape[1]), BF16)] * 2
    flops = 2 * 2 * count * q.shape[1] * blocks * block * 2
    if mode != "early":
        flops += 4 * count * weight.size
    vmem = pl.BlockSpec(memory_space=pltpu.VMEM)
    smem = pl.BlockSpec(memory_space=pltpu.SMEM)
    scalars = [] if mode == "late" else [block_valid]
    return pl.pallas_call(
        functools.partial(kernel_body, mode, scale, levels, turn, offset, count),
        in_specs=[smem] * len(scalars) + [vmem] * len(operands),
        out_specs=[vmem] * len(shapes),
        out_shape=shapes,
        scratch_shapes=[pltpu.VMEM((blocks * block, 2 * head_size), BF16)],
        cost_estimate=pl.CostEstimate(
            flops=flops,
            bytes_accessed=sum(x.size * x.dtype.itemsize for x in operands),
            transcendentals=2 * count * heads * blocks * block,
        ),
        compiler_params=pltpu.CompilerParams(vmem_limit_bytes=32 * MIB),
    )(*scalars, *operands)


def finish_kernel(keep_ref, got_ref, *refs):
    out_ref = refs[-1]
    start = 0
    for ref in refs[:-1]:
        stop = start + ref.shape[0]
        total = keep_ref[start:stop, :].astype(F32) + got_ref[start:stop, :].astype(F32)
        for i in range(ref.shape[1] // keep_ref.shape[1]):
            width = keep_ref.shape[1]
            total = total + ref[:, i * width : (i + 1) * width].astype(F32)
        out_ref[start:stop, :] = total.astype(BF16)
        start = stop


def finish(keep, got, others):
    return pl.pallas_call(
        finish_kernel,
        in_specs=[pl.BlockSpec(memory_space=pltpu.VMEM)] * (2 + len(others)),
        out_specs=pl.BlockSpec(memory_space=pltpu.VMEM),
        out_shape=jax.ShapeDtypeStruct(keep.shape, BF16),
        cost_estimate=pl.CostEstimate(flops=3 * keep.size, bytes_accessed=8 * keep.size, transcendentals=0),
        compiler_params=pltpu.CompilerParams(vmem_limit_bytes=16 * MIB),
        name="finish",
    )(keep, got, *others)


def cycle(block, axis, distance, first=0):
    count = lax.axis_size(axis) - first
    return lax.ppermute(
        block, axis, [(first + i, first + (i + distance) % count) for i in range(count)]
    )


def swapped(block, axis):
    return lax.ppermute(block, axis, [(i, i ^ 1) for i in range(lax.axis_size(axis))])


def per_device(queries, key_block, value_block, block_valid, out_weight):
    head_size = key_block.shape[1]
    ctx_size = lax.axis_size("ctx")
    kvh_size = lax.axis_size("kvh")
    block_id = lax.axis_index("ctx")
    levels = (ctx_size - 1).bit_length()
    scale = head_size ** (-0.5) * math.log2(math.e)
    count = queries.shape[0] // kvh_size
    groups = kvh_size // 2

    keys, values = [None] * levels, [None] * levels
    odd = block_id % 2 == 1
    keys[1] = cycle(key_block, "ctx", 2)
    values[1] = cycle(value_block, "ctx", 2)
    queries, key_block, value_block, out_weight = stage(queries, key_block, value_block, out_weight)
    for own, moved in ((key_block, keys), (value_block, values)):
        for level in range(2, levels):
            hop = 1 << (level - 1)
            moved[level] = cycle(moved[level - 1], "ctx", hop, hop)
        moved[0] = swapped(jnp.where(odd, moved[1], own), "ctx")
    rest = [0] + list(range(2, levels))
    piece = count // CHUNKS

    arrived = [[] for _ in range(CHUNKS)]
    for turn in range(1, groups):
        route = [(i, ((i // 2 + turn) % groups) * 2 + i % 2) for i in range(kvh_size)]
        (state,) = call(
            "early", scale, [None, 1], turn, 0, count, block_valid, queries, None, None,
            [key_block, keys[1]], [value_block, values[1]],
        )
        for j in range(CHUNKS):
            send, keep = call(
                "late", scale, rest, turn, j * piece, piece, block_valid, queries, state, out_weight,
                [keys[i] for i in rest], [values[i] for i in rest],
            )
            got = swapped(send, "kvh")
            both = (keep.astype(F32) + got.astype(F32)).astype(BF16)
            arrived[j].append(lax.ppermute(both, "kvh", route))
    send, keep = call(
        "full", scale, [None, 1] + rest, 0, 0, count, block_valid, queries, None, out_weight,
        [key_block, keys[1]] + [keys[i] for i in rest], [value_block, values[1]] + [values[i] for i in rest],
    )
    got = swapped(send, "kvh")
    return finish(keep, got, [x[0] if len(x) == 1 else jnp.concatenate(x, axis=1) for x in arrived])


def solution(mesh):
    return jax.shard_map(
        per_device,
        mesh=mesh,
        in_specs=(P("ctx", "kvh"), P("ctx", "kvh"), P("ctx", "kvh"), P(), P("kvh", None)),
        out_specs=P(("ctx", "kvh"), None),
        check_vma=False,
    )
```
